256 devices in a mesh: dp: 16 (over z, core), tensor: 4 (over y), corpus: 4 (over x).
Axes of the slice: x: 4, y: 4, z: 8, core: 2. Of those that a mesh axis runs over, the one named last changes fastest.
Arguments:
- queries: bfloat16 [4096, 2048], P(('dp', 'tensor', 'corpus')), may hold values from -24 to 24
- passages: bfloat16 [65536, 2048], P(('dp', 'corpus'), 'tensor'), may hold values from -6 to 6
- pos_ids: int32 [4096], P(('dp', 'tensor', 'corpus')), may hold values from 0 to 65535, as said below
- neg_ids: int32 [4096, 32], P(('dp', 'tensor', 'corpus')), may hold values from 0 to 65535, as said below
Outputs:
- grad_query: float32 [4096, 2048], P(('dp', 'tensor', 'corpus'))
- losses: float32 [4096], P(('dp', 'tensor', 'corpus'))
- grad_pass: float32 [65536, 2048], P(('dp', 'corpus'), 'tensor')
The draws below stay inside these ranges and needn't reach their ends.
Inputs may be any that keep to these rules, and one draw needn't show every extreme that they name: `pos_ids`: together with neg_ids: the ids named by the 16 queries of one device, positives and negatives together, fall at most 16 times into one block of 1024 passage rows (rows b * 1024 to (b + 1) * 1024 - 1), and exactly 16 times into one block that is the same for every device. Ids may repeat. `neg_ids`: counted together with pos_ids as stated there.
All inputs are finite; a program needn't handle non-finite values.
Results may differ from the reference program's by a relative error of at most 0.0035.
Values may be sent and summed in bfloat16 or wider, within the bound.
A program may use at most 128 MiB of HBM per device.

```python
import jax
import jax.numpy as jnp
from jax import lax

D = 2048
K = 32
QD = 16
OWNERS = 64
PB = 1024
CAP = 16
Q = 4096
P_SIZE = 65536
N_DP = 16
N_TENSOR = 4
N_CORPUS = 4


def request_ids(key):
    base_key = jax.random.fold_in(key, 11)
    pick_key, block_key = jax.random.split(base_key)
    busiest = jax.random.randint(pick_key, (), 0, OWNERS)
    slot_total = QD * (K + 1)

    def one_block(part_key):
        key_pool, key_mix, key_local = jax.random.split(part_key, 3)
        others = jnp.arange((OWNERS - 1) * CAP, dtype=jnp.int32) // CAP
        others = (others + busiest + 1) % OWNERS
        others = jax.random.permutation(key_pool, others)[:slot_total - CAP]
        owner_ids = jnp.concatenate([jnp.full((CAP,), busiest, jnp.int32), others.astype(jnp.int32)])
        owner_ids = jax.random.permutation(key_mix, owner_ids)
        local_ids = jax.random.randint(key_local, (slot_total,), 0, PB)
        return (owner_ids * PB + local_ids).reshape(QD, K + 1)
    block_keys = jax.random.split(block_key, Q // QD)
    return jax.vmap(one_block)(block_keys).reshape(Q, K + 1).astype(jnp.int32)


def passage_values(key):
    value_key = jax.random.fold_in(key, 23)
    return jnp.clip(jax.random.normal(value_key, (P_SIZE, D), jnp.float32), -6.0, 6.0)


def draw_passages(key, part):
    return passage_values(key).astype(jnp.bfloat16)


def draw_queries(key, part):
    noise_key = jax.random.fold_in(key, 31)
    values = jnp.clip(jax.random.normal(noise_key, (Q, D), jnp.float32), -6.0, 6.0)
    return values.astype(jnp.bfloat16)


def draw_pos_ids(key, part):
    return request_ids(key)[:, 0]


def draw_neg_ids(key, part):
    return request_ids(key)[:, 1:]


def setup_inputs(seed: int = 0) -> dict:
    key_of = jax.random.split(jax.random.key(seed), 5)
    return {
        "queries": draw_queries(jax.random.fold_in(key_of[4], 71), 0),
        "passages": draw_passages(jax.random.fold_in(key_of[4], 71), 0),
        "pos_ids": draw_pos_ids(jax.random.fold_in(key_of[4], 71), 0),
        "neg_ids": draw_neg_ids(jax.random.fold_in(key_of[4], 71), 0),
    }


def regroup(values):
    shaped = values.reshape((N_DP, N_TENSOR * N_CORPUS, QD) + values.shape[1:])
    shaped = jnp.swapaxes(shaped, 0, 1)
    return shaped.reshape((N_TENSOR * N_CORPUS, N_DP * QD) + values.shape[1:])


def ungroup(values):
    shaped = values.reshape((N_TENSOR * N_CORPUS, N_DP, QD) + values.shape[2:])
    shaped = jnp.swapaxes(shaped, 0, 1)
    return shaped.reshape((Q,) + values.shape[2:])


def reference(queries, passages, pos_ids, neg_ids):
    score_scale = D ** -0.5
    columns = N_DP * QD

    def group_step(grad_pass, group):
        query_rows, pos_group, neg_group = group
        pos_rows = jnp.take(passages, pos_group, axis=0)
        neg_rows = jnp.take(passages, neg_group, axis=0)
        in_scores = jnp.dot(query_rows, pos_rows.T, preferred_element_type=jnp.float32) * score_scale
        neg_scores = jnp.einsum("md,mkd->mk", query_rows.astype(jnp.float32), neg_rows.astype(jnp.float32)) * score_scale
        logits = jnp.concatenate([in_scores, neg_scores], axis=1)
        row_max = jnp.max(logits, axis=1, keepdims=True)
        exponent = jnp.exp(logits - row_max)
        denominator = jnp.sum(exponent, axis=1, keepdims=True)
        target = (jnp.arange(columns + K)[None, :] == jnp.arange(columns)[:, None]).astype(jnp.float32)
        losses = jnp.log(denominator[:, 0]) + row_max[:, 0] - jnp.sum(target * logits, axis=1)
        weights = (exponent / denominator - target).astype(jnp.bfloat16)
        in_weights = weights[:, :columns]
        neg_weights = weights[:, columns:]
        grad_query = jnp.dot(in_weights, pos_rows, preferred_element_type=jnp.float32)
        grad_query = grad_query + jnp.einsum("mk,mkd->md", neg_weights.astype(jnp.float32), neg_rows.astype(jnp.float32))
        grad_query = grad_query * score_scale
        pos_grad = jnp.dot(in_weights.T, query_rows, preferred_element_type=jnp.float32) * score_scale
        neg_grad = neg_weights.astype(jnp.float32)[:, :, None] * query_rows.astype(jnp.float32)[:, None, :] * score_scale
        row_grads = jnp.concatenate([pos_grad[:, None, :], neg_grad], axis=1).astype(jnp.bfloat16)
        row_grads = lax.optimization_barrier(row_grads).astype(jnp.float32)
        named_ids = jnp.concatenate([pos_group[:, None], neg_group], axis=1).reshape(-1)
        grad_pass = grad_pass.at[named_ids].add(row_grads.reshape(-1, D))
        return grad_pass, (grad_query, losses)

    grad_pass, outputs = lax.scan(group_step, jnp.zeros((P_SIZE, D), jnp.float32), (regroup(queries), regroup(pos_ids), regroup(neg_ids)))
    grad_query, losses = outputs
    return (ungroup(grad_query), ungroup(losses), grad_pass)
```

```python
import jax
import jax.numpy as jnp
from jax import lax
from jax.sharding import PartitionSpec as P

CAP = 16


def gather_queries(queries):
    n_dp, n_t, n_c = (lax.axis_size(a) for a in ("dp", "tensor", "corpus"))
    qd, feat = queries.shape
    width = feat // n_t
    mine = queries.reshape(qd, n_t, width).swapaxes(0, 1)
    mine = lax.all_to_all(mine, "tensor", split_axis=0, concat_axis=0, tiled=True)
    every = lax.all_gather(mine, ("dp", "corpus"), axis=0, tiled=False)
    every = every.reshape(n_dp, n_c, n_t, qd, width).transpose(2, 1, 0, 3, 4)
    return every.reshape(n_t * n_c, n_dp * qd, width)


def gather_small(values):
    n_dp, n_t, n_c = (lax.axis_size(a) for a in ("dp", "tensor", "corpus"))
    every = lax.all_gather(values, ("dp", "tensor", "corpus"), axis=0, tiled=False)
    every = every.reshape((n_dp, n_t * n_c) + values.shape)
    return jnp.swapaxes(every, 0, 1)


def scatter_scores(part):
    n_groups, n_dp = part.shape[:2]
    part = jnp.swapaxes(part, 0, 1).reshape((n_dp * n_groups,) + part.shape[2:])
    return lax.psum_scatter(part, ("dp", "tensor", "corpus"), scatter_dimension=0, tiled=False)


def scatter_grads(part):
    n_dp, n_t, n_c = (lax.axis_size(a) for a in ("dp", "tensor", "corpus"))
    n_groups, members, width = part.shape
    qd = members // n_dp
    part = part.reshape(n_t, n_c, n_dp, qd, width).transpose(2, 1, 0, 3, 4)
    part = part.reshape(n_dp * n_c, n_t, qd, width)
    mine = lax.psum_scatter(part, ("dp", "corpus"), scatter_dimension=0, tiled=False)
    mine = lax.all_to_all(mine, "tensor", split_axis=0, concat_axis=0, tiled=True)
    return mine.swapaxes(0, 1).reshape(qd, n_t * width)


def body(queries, passages, pos_ids, neg_ids):
    n_dp, n_t, n_c = (lax.axis_size(a) for a in ("dp", "tensor", "corpus"))
    qd, feat = queries.shape
    block_rows, width = passages.shape
    neg_count = neg_ids.shape[1]
    n_groups = n_t * n_c
    members = n_dp * qd
    items = (neg_count + 1) * qd
    scale = feat ** (-0.5)
    f32, bf16 = jnp.float32, jnp.bfloat16
    block = lax.axis_index("dp") * n_c + lax.axis_index("corpus")

    ids = jnp.concatenate([pos_ids[None, :], neg_ids.T], axis=0).reshape(items)
    every_id = gather_small(ids)
    every_query = gather_queries(queries)

    item_no = jnp.arange(items, dtype=jnp.int32)
    match = every_id // block_rows == block
    before = (item_no[:, None] < item_no[None, :]).astype(bf16)
    rank = jnp.einsum("gdj,jk->gdk", match.astype(bf16), before, preferred_element_type=f32)
    rank = jnp.where(match, rank.astype(jnp.int32), -1)
    packed = (every_id % block_rows) * items + item_no + 1
    slot_no = jnp.arange(CAP, dtype=jnp.int32)
    held = jnp.sum(
        jnp.where(rank[:, :, None, :] == slot_no[:, None], packed[:, :, None, :], 0), axis=3
    )
    full = held > 0
    row = jnp.where(full, (held - 1) // items, -1)
    item = jnp.where(full, (held - 1) % items, -1)
    slots = n_dp * CAP
    own = jnp.arange(n_dp, dtype=jnp.int32)[:, None] * qd + item % qd
    own = jnp.where(full, own, -1).reshape(n_groups, slots)
    is_pos = (full & (item < qd)).reshape(n_groups, slots)
    member_no = jnp.arange(members, dtype=jnp.int32)
    onehot = (row.reshape(n_groups, slots)[:, :, None] == jnp.arange(block_rows)).astype(bf16)
    at_own = own[:, :, None] == member_no
    pick_pos = (at_own & is_pos[:, :, None]).astype(bf16)
    at_neg = at_own & ~is_pos[:, :, None]

    rows = jnp.einsum("gsp,pw->gsw", onehot, passages, preferred_element_type=f32).astype(bf16)
    pos_rows = jnp.einsum("gsc,gsw->gcw", pick_pos, rows, preferred_element_type=f32).astype(bf16)
    in_part = jnp.einsum("gqw,gcw->gqc", every_query, pos_rows, preferred_element_type=f32)
    slot_part = jnp.einsum("gsw,gqw->gsq", rows, every_query, preferred_element_type=f32)
    score = jnp.sum(jnp.where(at_neg, slot_part, 0.0), axis=2).reshape(n_groups, n_dp, CAP)
    neg_no = item_no[qd:]
    neg_part = jnp.sum(
        jnp.where(item[:, :, :, None] == neg_no, score[:, :, :, None], 0.0), axis=2
    )
    neg_part = neg_part.reshape(n_groups, n_dp, neg_count, qd).swapaxes(2, 3)
    part = jnp.concatenate([in_part.reshape(n_groups, n_dp, qd, members), neg_part], axis=3)
    logits = scatter_scores(part) * scale

    row_max = jnp.max(logits, axis=1, keepdims=True)
    exponent = jnp.exp(logits - row_max)
    denominator = jnp.sum(exponent, axis=1, keepdims=True)
    own_col = lax.axis_index("dp") * qd + jnp.arange(qd)
    target = (jnp.arange(members + neg_count)[None, :] == own_col[:, None]).astype(f32)
    losses = jnp.log(denominator[:, 0]) + row_max[:, 0] - jnp.sum(target * logits, axis=1)
    weights = (exponent / denominator - target).astype(bf16)

    every_weight = gather_small(weights)
    in_weights = every_weight[..., :members].reshape(n_groups, members, members)
    neg_weights = every_weight[..., members:].swapaxes(2, 3).reshape(n_groups, n_dp, -1)
    slot_weight = jnp.sum(
        jnp.where(
            item[:, :, :, None] == neg_no, neg_weights[:, :, None, :].astype(f32), 0.0
        ),
        axis=3,
    ).reshape(n_groups, slots)
    spread = jnp.einsum("gsc,gqc->gsq", pick_pos, in_weights, preferred_element_type=f32)
    spread = jnp.where(at_neg, slot_weight[:, :, None], spread).astype(bf16)
    slot_grads = jnp.einsum("gsq,gqw->gsw", spread, every_query, preferred_element_type=f32)
    slot_grads = (slot_grads * scale).astype(bf16)
    grad_pass = jnp.einsum("gsp,gsw->pw", onehot, slot_grads, preferred_element_type=f32)
    query_part = jnp.einsum("gsq,gsw->gqw", spread, rows, preferred_element_type=f32)
    grad_query = scatter_grads(query_part * scale)
    return (grad_query, losses, grad_pass)


def solution(mesh):
    in_specs = (
        P(("dp", "tensor", "corpus"), None),
        P(("dp", "corpus"), "tensor"),
        P(("dp", "tensor", "corpus")),
        P(("dp", "tensor", "corpus"), None),
    )
    out_specs = (
        P(("dp", "tensor", "corpus"), None),
        P(("dp", "tensor", "corpus")),
        P(("dp", "corpus"), "tensor"),
    )
    return jax.shard_map(body, mesh=mesh, in_specs=in_specs, out_specs=out_specs, check_vma=False)
```

```python
import functools

import jax
import jax.numpy as jnp
from jax import lax
from jax.experimental import pallas as pl
from jax.experimental.pallas import tpu as pltpu
from jax.sharding import PartitionSpec as P

CAP = 16
VMEM_LIMIT = 62 * 1024 * 1024
CORES = 2


class Place:
    def __init__(self):
        dp = lax.axis_index("dp")
        self.size = {
            "z": lax.axis_size("dp") // CORES,
            "tensor": lax.axis_size("tensor"),
            "corpus": lax.axis_size("corpus"),
        }
        self.at = {
            "z": dp // CORES,
            "tensor": lax.axis_index("tensor"),
            "corpus": lax.axis_index("corpus"),
        }
        self.core = dp % CORES

    def along(self, axis, step):
        n = self.size[axis]
        return lax.rem(self.at[axis] + (step + n), n)

    def device(self, axis, step):
        if axis == "core":
            return {"dp": self.at["z"] * CORES + (1 - self.core)}
        spot = self.along(axis, step)
        if axis == "z":
            return {"dp": spot * CORES + self.core}
        return {axis: spot}

    def greet(self, peers):
        barrier = pltpu.get_barrier_semaphore()
        for axis, step in peers:
            pl.semaphore_signal(
                barrier, inc=1, device_id=self.device(axis, step),
                device_id_type=pl.DeviceIdType.MESH,
            )
        pl.semaphore_wait(barrier, len(peers))


class Wire:
    def __init__(self, send_sem, recv_sem):
        self.send_sem, self.recv_sem = send_sem, recv_sem
        self.used = 0
        self.sent = []

    def make(self, src, dst, device, number):
        return pltpu.make_async_remote_copy(
            src_ref=src, dst_ref=dst, send_sem=self.send_sem.at[number],
            recv_sem=self.recv_sem.at[number], device_id=device,
            device_id_type=pl.DeviceIdType.MESH,
        )

    def send(self, src, dst, device, landing):
        number = self.used
        self.used += 1
        copy = self.make(src, dst, device, number)
        copy.start()
        self.sent.append(copy)
        return self.make(landing, landing, device, number)

    def finish(self):
        for copy in self.sent:
            copy.wait_send()


def interleave(walks):
    walks = list(walks)
    while walks:
        for walk in list(walks):
            try:
                next(walk)
            except StopIteration:
                walks.remove(walk)


def add_to(dst, first, others):
    lead = 1
    for n in dst.shape[:-2]:
        lead *= n
    if len(dst.shape) > 2 and lead * dst.shape[-2] * dst.shape[-1] > 32 * 1024:
        def step(i, carry):
            add_to(dst.at[i], first.at[i], [o.at[i] for o in others])
            return carry
        lax.fori_loop(0, dst.shape[0], step, 0)
        return
    total = first[...]
    for o in others:
        total = total + o[...]
    dst[...] = total


def ring_gather(place, wire, view, axes, flip, swap):
    for stage, axis in enumerate(axes):
        n = place.size[axis]
        last = stage == len(axes) - 1
        def at(step, axis=axis, stage=stage):
            where = {}
            for a in axes[:stage]:
                where[a] = slice(None)
            where[axis] = place.along(axis, step)
            for a in axes[stage + 1:]:
                where[a] = place.at[a]
            return where
        far = n // 2
        near = n - 1 - far
        hops = {1: near, -1: far} if flip else {1: far, -1: near}
        if last:
            swap(at(0))
        landed = {1: None, -1: None}
        for s in range(far):
            for way in (1, -1):
                if s < hops[way]:
                    if landed[way] is not None:
                        landed[way].wait_recv()
                        if last:
                            swap(at(-way * s))
                    block = view(at(-way * s), place.core)
                    coming = view(at(-way * (s + 1)), place.core)
                    landed[way] = wire.send(block, block, place.device(axis, way), coming)
            yield
        for way in (1, -1):
            if landed[way] is not None:
                landed[way].wait_recv()
                if last:
                    swap(at(-way * hops[way]))
        yield


def ring_reduce(place, wire, held, dims, axes, boxes, holds, flip, out):
    dims = list(dims)
    for stage, axis in enumerate(axes):
        n = place.size[axis]
        spot = dims.index(axis)

        def at(step, held=held, spot=spot, axis=axis):
            return held.at[(slice(None),) * spot + (place.along(axis, step),)]

        box = boxes[stage]
        far = n // 2
        near = n - 1 - far
        hops = {1: near, -1: far} if flip else {1: far, -1: near}
        base = {1: 0, -1: hops[1]}
        landed = {}
        for s in range(far):
            for way in (1, -1):
                if s < hops[way]:
                    source = at(way * (hops[way] - s))
                    if s > 0:
                        landed[way].wait_recv()
                        got = box.at[base[way] + s - 1]
                        add_to(got, got, [source])
                        source = got
                    slot = box.at[base[way] + s]
                    landed[way] = wire.send(source, slot, place.device(axis, way), slot)
            yield
        terms = []
        for way in (1, -1):
            if hops[way]:
                landed[way].wait_recv()
                terms.append(box.at[base[way] + hops[way] - 1])
        target = out if stage == len(axes) - 1 else holds[stage]
        add_to(target, at(0), terms)
        held = target
        dims.pop(spot)
        yield


def fold_cores(place, wire, part, box, lead):
    every = (slice(None),) * lead
    landing = wire.send(part.at[every + (1 - place.core,)], box, place.device("core", 1), box)
    yield
    landing.wait_recv()
    add_to(box, box, [part.at[every + (place.core,)]])
    yield


def reduce_walk(place, wire, part, box, dims, axes, boxes, holds, flip, out):
    yield from fold_cores(place, wire, part, box, len(dims))
    yield from ring_reduce(place, wire, box, dims, axes, boxes, holds, flip, out)


def reduce_scratch(sizes, dims, axes, chunk):
    def buffer(lead):
        return pltpu.VMEM(tuple(lead) + tuple(chunk), jnp.float32)

    left = list(dims)
    fold = buffer([sizes[d] for d in left])
    boxes, holds = [], []
    for stage, axis in enumerate(axes):
        left.remove(axis)
        part = [sizes[d] for d in left]
        boxes.append(buffer([sizes[axis] - 1] + part))
        if stage < len(axes) - 1:
            holds.append(buffer(part))
    return [fold] + boxes + holds


def split_scratch(refs, stages):
    return refs[0], refs[1:1 + stages], refs[1 + stages:2 * stages]


def mesh_sizes():
    return {
        "z": lax.axis_size("dp") // CORES,
        "tensor": lax.axis_size("tensor"),
        "corpus": lax.axis_size("corpus"),
    }


def ring_peers(axes):
    return [("core", 1)] + [(a, way) for a in axes for way in (1, -1)]


VMEM_SPEC = pl.BlockSpec(memory_space=pltpu.VMEM)


def kernel_call(kernel, outs, scratch, copies, number, inputs):
    return pl.pallas_call(
        kernel,
        out_shape=outs,
        in_specs=[VMEM_SPEC] * len(inputs),
        out_specs=[VMEM_SPEC] * len(outs),
        scratch_shapes=[
            pltpu.SemaphoreType.DMA((copies,)),
            pltpu.SemaphoreType.DMA((copies,)),
        ] + scratch,
        compiler_params=pltpu.CompilerParams(
            collective_id=number, has_side_effects=True, vmem_limit_bytes=VMEM_LIMIT
        ),
    )(*inputs)


def swapper(place, wire, view, waits):
    def swap(where):
        block = view(where, place.core)
        landing = view(where, 1 - place.core)
        waits.append(wire.send(block, block, place.device("core", 1), landing))
    return swap


def query_kernel(q_in, ids_in, q_out, ids_out, send_sem, recv_sem, own_sem):
    place = Place()
    wire = Wire(send_sem, recv_sem)
    n_t = place.size["tensor"]
    t, c, z, core = place.at["tensor"], place.at["corpus"], place.at["z"], place.core
    place.greet(ring_peers(("z", "corpus")) + [("tensor", o) for o in range(1, n_t)])
    keep = [
        pltpu.make_async_copy(q_in.at[t], q_out.at[t, c, z, core], own_sem.at[0]),
        pltpu.make_async_copy(ids_in, ids_out.at[t, c, z, core], own_sem.at[1]),
    ]
    for copy in keep:
        copy.start()
    landings = []
    for o in range(1, n_t):
        peer, source = place.along("tensor", o), place.along("tensor", -o)
        device = place.device("tensor", o)
        landings.append(wire.send(
            q_in.at[peer], q_out.at[t, c, z, core], device, q_out.at[source, c, z, core]
        ))
        landings.append(wire.send(
            ids_in, ids_out.at[t, c, z, core], device, ids_out.at[source, c, z, core]
        ))
    for copy in keep:
        copy.wait()
    for landing in landings:
        landing.wait_recv()
    half = n_t // 2

    def of(ref, part):
        return lambda where, k: ref.at[part, where["corpus"], where["z"], k]

    waits, walks = [], []
    for ref, part, axes, flip in (
        (ids_out, slice(0, n_t), ("corpus", "z"), True),
        (q_out, slice(0, half), ("corpus", "z"), False),
        (q_out, slice(half, n_t), ("z", "corpus"), True),
    ):
        view = of(ref, part)
        walks.append(ring_gather(
            place, wire, view, axes, flip, swapper(place, wire, view, waits)
        ))
    interleave(walks)
    for landing in waits:
        landing.wait_recv()
    wire.finish()


def gather_queries(queries, ids):
    sizes = mesh_sizes()
    n_t, n_c, n_z = sizes["tensor"], sizes["corpus"], sizes["z"]
    qd, feat = queries.shape
    width = feat // n_t
    mine = queries.reshape(qd, n_t, width).swapaxes(0, 1)
    lead = (n_t, n_c, n_z, CORES)
    count = ids.shape[1]
    copies = 2 * (n_t - 1) + 3 * (n_c + n_z - 2) + 2 * n_z + n_c
    every_query, every_id = kernel_call(
        query_kernel,
        [
            jax.ShapeDtypeStruct(lead + (qd, width), queries.dtype),
            jax.ShapeDtypeStruct(lead + (1, count), ids.dtype),
        ],
        [pltpu.SemaphoreType.DMA((2,))], copies, 0, (mine, ids),
    )
    groups, members = n_t * n_c, n_z * CORES
    return (
        every_query.reshape(groups, members * qd, width),
        every_id.reshape(groups, members, count),
    )


WEIGHT_WALKS = (
    (("tensor", "corpus", "z"), False),
    (("z", "tensor", "corpus"), True),
    (("corpus", "z", "tensor"), False),
)


def weight_kernel(*refs):
    parts = len(WEIGHT_WALKS)
    ins, outs = refs[:parts], refs[parts:2 * parts]
    send_sem, recv_sem, own_sem = refs[2 * parts:]
    place = Place()
    wire = Wire(send_sem, recv_sem)
    t, c, z, core = place.at["tensor"], place.at["corpus"], place.at["z"], place.core
    place.greet(ring_peers(("z", "corpus", "tensor")))
    keep = [
        pltpu.make_async_copy(i, o.at[t, c, z, core], own_sem.at[n])
        for n, (i, o) in enumerate(zip(ins, outs))
    ]
    for copy in keep:
        copy.start()
    for copy in keep:
        copy.wait()

    def of(ref):
        return lambda where, k: ref.at[where["tensor"], where["corpus"], where["z"], k]

    waits, walks = [], []
    for out, (axes, flip) in zip(outs, WEIGHT_WALKS):
        view = of(out)
        walks.append(ring_gather(
            place, wire, view, axes, flip, swapper(place, wire, view, waits)
        ))
    interleave(walks)
    for landing in waits:
        landing.wait_recv()
    wire.finish()


def gather_weights(parts):
    sizes = mesh_sizes()
    lead = (sizes["tensor"], sizes["corpus"], sizes["z"], CORES)
    hops = sum(sizes.values()) - 3
    copies = sum(hops + sizes[axes[-1]] for axes, _ in WEIGHT_WALKS)
    return kernel_call(
        weight_kernel,
        [jax.ShapeDtypeStruct(lead + p.shape, p.dtype) for p in parts],
        [pltpu.SemaphoreType.DMA((len(parts),))], copies, 1, tuple(parts),
    )


SCORE_DIMS = ("tensor", "corpus", "z")
SCORE_WALKS = (
    (("tensor", "z", "corpus"), False),
    (("z", "corpus", "tensor"), True),
    (("corpus", "tensor", "z"), False),
)


def score_kernel(*refs):
    parts = len(SCORE_WALKS)
    ins, outs = refs[:parts], refs[parts:2 * parts]
    send_sem, recv_sem = refs[2 * parts:2 * parts + 2]
    scratch = refs[2 * parts + 2:]
    place = Place()
    wire = Wire(send_sem, recv_sem)
    place.greet(ring_peers(SCORE_DIMS))
    each = len(scratch) // parts
    walks = []
    for n, (axes, flip) in enumerate(SCORE_WALKS):
        fold, boxes, holds = split_scratch(scratch[n * each:(n + 1) * each], len(axes))
        walks.append(reduce_walk(
            place, wire, ins[n], fold, SCORE_DIMS, axes, boxes, holds, flip, outs[n]
        ))
    interleave(walks)
    wire.finish()


def scatter_scores(parts):
    sizes = mesh_sizes()
    scratch = []
    chunks = [p.shape[4:] for p in parts]
    for chunk, (axes, _) in zip(chunks, SCORE_WALKS):
        scratch += reduce_scratch(sizes, SCORE_DIMS, axes, chunk)
    copies = len(parts) * (sum(sizes.values()) - 2)
    return kernel_call(
        score_kernel, [jax.ShapeDtypeStruct(c, jnp.float32) for c in chunks],
        scratch, copies, 2, tuple(parts),
    )


GRAD_DIMS = ("corpus", "z")
GRAD_WALKS = ((("corpus", "z"), False), (("z", "corpus"), True))


def grad_kernel(*refs):
    parts = len(GRAD_WALKS)
    ins, out = refs[:parts], refs[parts]
    send_sem, recv_sem, own_sem, done = refs[parts + 1:parts + 5]
    scratch = refs[parts + 5:]
    place = Place()
    wire = Wire(send_sem, recv_sem)
    n_t, t = place.size["tensor"], place.at["tensor"]
    place.greet(ring_peers(GRAD_DIMS) + [("tensor", o) for o in range(1, n_t)])
    each = len(scratch) // parts
    share = n_t // parts
    walks = []
    for n, (axes, flip) in enumerate(GRAD_WALKS):
        fold, boxes, holds = split_scratch(scratch[n * each:(n + 1) * each], len(axes))
        walks.append(reduce_walk(
            place, wire, ins[n], fold, GRAD_DIMS, axes, boxes, holds, flip,
            done.at[n * share:(n + 1) * share],
        ))
    interleave(walks)
    keep = pltpu.make_async_copy(done.at[t], out.at[t], own_sem.at[0])
    keep.start()
    landings = []
    for o in range(1, n_t):
        peer, source = place.along("tensor", o), place.along("tensor", -o)
        landings.append(wire.send(
            done.at[peer], out.at[t], place.device("tensor", o), out.at[source]
        ))
    keep.wait()
    for landing in landings:
        landing.wait_recv()
    wire.finish()


def scatter_grads(parts):
    sizes = mesh_sizes()
    share, qd, width = parts[0].shape[3:]
    n_t = sizes["tensor"]
    scratch = [pltpu.SemaphoreType.DMA((1,)), pltpu.VMEM((n_t, qd, width), jnp.float32)]
    for axes, _ in GRAD_WALKS:
        scratch += reduce_scratch(sizes, GRAD_DIMS, axes, (share, qd, width))
    copies = len(parts) * (sizes["corpus"] + sizes["z"] - 1) + n_t - 1
    (mine,) = kernel_call(
        grad_kernel, [jax.ShapeDtypeStruct((n_t, qd, width), jnp.float32)],
        scratch, copies, 3, tuple(parts),
    )
    return mine.swapaxes(0, 1).reshape(qd, n_t * width)


def body(queries, passages, pos_ids, neg_ids):
    sizes = mesh_sizes()
    n_t, n_c, n_z = sizes["tensor"], sizes["corpus"], sizes["z"]
    n_dp = n_z * CORES
    qd, feat = queries.shape
    block_rows, width = passages.shape
    neg_count = neg_ids.shape[1]
    n_groups = n_t * n_c
    members = n_dp * qd
    items = (neg_count + 1) * qd
    padded = -(-(items + 1) // 128) * 128
    scale = feat ** (-0.5)
    f32, bf16 = jnp.float32, jnp.bfloat16
    block = lax.axis_index("dp") * n_c + lax.axis_index("corpus")
    lead = (n_t, n_c, n_z, CORES)

    ids = jnp.concatenate([pos_ids[None, :], neg_ids.T], axis=0).reshape(1, items)
    ids = jnp.pad(ids, ((0, 0), (0, padded - items)), constant_values=-1)
    every_query, every_id = gather_queries(queries, ids)

    item_no = jnp.arange(padded, dtype=jnp.int32)
    match = every_id // block_rows == block
    before = (item_no[:, None] < item_no[None, :]).astype(bf16)
    rank = jnp.einsum("gdj,jk->gdk", match.astype(bf16), before, preferred_element_type=f32)
    rank = jnp.where(match, rank.astype(jnp.int32), -1)
    packed = (every_id % block_rows) * padded + item_no + 1
    slot_no = jnp.arange(CAP, dtype=jnp.int32)
    held = jnp.sum(
        jnp.where(rank[:, :, None, :] == slot_no[:, None], packed[:, :, None, :], 0), axis=3
    )
    full = held > 0
    row = jnp.where(full, (held - 1) // padded, -1)
    item = jnp.where(full, (held - 1) % padded, -1)
    slots = n_dp * CAP
    own = jnp.arange(n_dp, dtype=jnp.int32)[:, None] * qd + item % qd
    own = jnp.where(full, own, -1).reshape(n_groups, slots)
    is_pos = (full & (item < qd)).reshape(n_groups, slots)
    member_no = jnp.arange(members, dtype=jnp.int32)
    onehot = (row.reshape(n_groups, slots)[:, :, None] == jnp.arange(block_rows)).astype(bf16)
    at_own = own[:, :, None] == member_no
    pick_pos = (at_own & is_pos[:, :, None]).astype(bf16)
    at_neg = at_own & ~is_pos[:, :, None]

    rows = jnp.einsum("gsp,pw->gsw", onehot, passages, preferred_element_type=f32).astype(bf16)
    pos_rows = jnp.einsum("gsc,gsw->gcw", pick_pos, rows, preferred_element_type=f32).astype(bf16)
    half = members // 2
    in_parts = [
        jnp.einsum("gqw,gcw->gqc", every_query, cols, preferred_element_type=f32)
        for cols in (pos_rows[:, :half], pos_rows[:, half:])
    ]
    slot_part = jnp.einsum("gsw,gqw->gsq", rows, every_query, preferred_element_type=f32)
    score = jnp.sum(jnp.where(at_neg, slot_part, 0.0), axis=2).reshape(n_groups, n_dp, CAP)
    neg_no = item_no[qd:items]
    neg_part = jnp.sum(
        jnp.where(item[:, :, :, None] == neg_no, score[:, :, :, None], 0.0), axis=2
    )
    neg_shape = (neg_count * qd // 128, 128)
    left, right, neg = scatter_scores([
        in_parts[0].reshape(lead + (qd, half)),
        in_parts[1].reshape(lead + (qd, half)),
        neg_part.reshape(lead + neg_shape),
    ])
    neg = neg.reshape(neg_count, qd).T
    logits = jnp.concatenate([left, right, neg], axis=1) * scale

    row_max = jnp.max(logits, axis=1, keepdims=True)
    exponent = jnp.exp(logits - row_max)
    denominator = jnp.sum(exponent, axis=1, keepdims=True)
    own_col = lax.axis_index("dp") * qd + jnp.arange(qd)
    target = (jnp.arange(members + neg_count)[None, :] == own_col[:, None]).astype(f32)
    losses = jnp.log(denominator[:, 0]) + row_max[:, 0] - jnp.sum(target * logits, axis=1)
    weights = (exponent / denominator - target).astype(bf16)

    left, right, neg = gather_weights([
        weights[:, :half],
        weights[:, half:members],
        weights[:, members:].T.astype(f32).reshape(neg_shape),
    ])
    neg_weights = neg.reshape(n_groups, n_dp, 1, neg_count * qd)
    slot_weight = jnp.sum(
        jnp.where(item[:, :, :, None] == neg_no, neg_weights, 0.0), axis=3
    ).reshape(n_groups, slots)
    spread = sum(
        jnp.einsum(
            "gsc,gqc->gsq", pick, w.reshape(n_groups, members, half), preferred_element_type=f32
        )
        for pick, w in ((pick_pos[..., :half], left), (pick_pos[..., half:], right))
    )
    spread = jnp.where(at_neg, slot_weight[:, :, None], spread).astype(bf16)
    share = n_t // len(GRAD_WALKS)
    group_share = share * n_c

    def query_part(first):
        part = jnp.einsum(
            "gsq,gsw->gqw", spread[first:first + group_share], rows[first:first + group_share],
            preferred_element_type=f32,
        ) * scale
        part = part.reshape((share, n_c * n_z * CORES, qd, width)).swapaxes(0, 1)
        return part.reshape(n_c, n_z, CORES, share, qd, width)

    grad_query = scatter_grads([query_part(n * group_share) for n in range(len(GRAD_WALKS))])
    slot_grads = jnp.einsum("gsq,gqw->gsw", spread, every_query, preferred_element_type=f32)
    slot_grads = (slot_grads * scale).astype(bf16)
    grad_pass = jnp.einsum("gsp,gsw->pw", onehot, slot_grads, preferred_element_type=f32)
    return (grad_query, losses, grad_pass)


def solution(mesh):
    in_specs = (
        P(("dp", "tensor", "corpus"), None),
        P(("dp", "corpus"), "tensor"),
        P(("dp", "tensor", "corpus")),
        P(("dp", "tensor", "corpus"), None),
    )
    out_specs = (
        P(("dp", "tensor", "corpus"), None),
        P(("dp", "tensor", "corpus")),
        P(("dp", "corpus"), "tensor"),
    )
    return jax.shard_map(body, mesh=mesh, in_specs=in_specs, out_specs=out_specs, check_vma=False)
```

```python
import heapq
import math

import jax
import jax.numpy as jnp
from jax import lax
from jax.experimental import pallas as pl
from jax.experimental.pallas import tpu as pltpu
from jax.sharding import PartitionSpec as P

CAP = 16
VMEM_LIMIT = 62 * 1024 * 1024
CORES = 2


class Place:
    def __init__(self):
        dp = lax.axis_index("dp")
        self.size = {
            "z": lax.axis_size("dp") // CORES,
            "tensor": lax.axis_size("tensor"),
            "corpus": lax.axis_size("corpus"),
        }
        self.at = {
            "z": dp // CORES,
            "tensor": lax.axis_index("tensor"),
            "corpus": lax.axis_index("corpus"),
        }
        self.core = dp % CORES

    def along(self, axis, step):
        n = self.size[axis]
        return lax.rem(self.at[axis] + (step + n), n)

    def device(self, axis, step):
        if axis == "core":
            return {"dp": self.at["z"] * CORES + (1 - self.core)}
        spot = self.along(axis, step)
        if axis == "z":
            return {"dp": spot * CORES + self.core}
        return {axis: spot}

    def greet(self, peers):
        barrier = pltpu.get_barrier_semaphore()
        for axis, step in peers:
            pl.semaphore_signal(
                barrier, inc=1, device_id=self.device(axis, step),
                device_id_type=pl.DeviceIdType.MESH,
            )
        pl.semaphore_wait(barrier, len(peers))


LINK_RATE = 90e3
SWAP_RATE = 450e3


class Flow:
    def __init__(self, send_sem, recv_sem):
        self.send_sem, self.recv_sem = send_sem, recv_sem
        self.used = 0
        self.sent = []
        self.coming = []
        self.now = 0.0
        self.busy = {}

    def make(self, src, dst, device, number):
        return pltpu.make_async_remote_copy(
            src_ref=src, dst_ref=dst, send_sem=self.send_sem.at[number],
            recv_sem=self.recv_sem.at[number], device_id=device,
            device_id_type=pl.DeviceIdType.MESH,
        )

    def post(self, src, dst, device, landing, link, hops, then=None):
        number = self.used
        self.used += 1
        copy = self.make(src, dst, device, number)
        copy.start()
        self.sent.append(copy)
        size = math.prod(src.shape) * jnp.dtype(src.dtype).itemsize
        cost = size / SWAP_RATE if link == "core" else CORES * hops * size / LINK_RATE
        begin = max(self.now, self.busy.get(link, 0.0))
        self.busy[link] = begin + cost
        due = begin + cost + 0.8 + 0.7 * hops
        self.now += 0.01
        heapq.heappush(
            self.coming, (due, number, self.make(landing, landing, device, number), then)
        )

    def run(self):
        while self.coming:
            due, _, landing, then = heapq.heappop(self.coming)
            self.now = max(self.now, due)
            landing.wait_recv()
            if then is not None:
                then()
        for copy in self.sent:
            copy.wait_send()


def add_to(dst, first, others):
    if len(dst.shape) > 2 and math.prod(dst.shape) > 32 * 1024:
        def step(i, carry):
            add_to(dst.at[i], first.at[i], [o.at[i] for o in others])
            return carry
        lax.fori_loop(0, dst.shape[0], step, 0)
        return
    total = first[...].astype(jnp.float32)
    for o in others:
        total = total + o[...].astype(jnp.float32)
    dst[...] = total.astype(dst.dtype)


def direct_link(axis, step, n):
    way = 1 if step <= n // 2 else -1
    return (axis, way), min(step, n - step)


def ring_hops(n, flip=False):
    far, near = n // 2, n - 1 - n // 2
    return {1: near, -1: far} if flip else {1: far, -1: near}


def relay(flow, place, view, where, axis, way, hop, hops, have):
    at = dict(where, **{axis: place.along(axis, -way * hop)})
    coming = dict(where, **{axis: place.along(axis, -way * (hop + 1))})
    block = view(at, place.core)

    def then():
        if hop + 1 < hops:
            relay(flow, place, view, where, axis, way, hop + 1, hops, have)
        have(coming)

    flow.post(
        block, block, place.device(axis, way), view(coming, place.core), (axis, way), 1, then
    )


def spread(flow, place, view, where, axes, ring, have):
    for i, axis in enumerate(axes):
        rest = axes[i + 1:]

        def went(coming, rest=rest):
            spread(flow, place, view, coming, rest, ring, have)

        n = place.size[axis]
        if ring is not None and n > 4:
            hops = ring_hops(n, ring)
            for way in (1, -1):
                if hops[way]:
                    relay(flow, place, view, where, axis, way, 0, hops[way], went)
        else:
            block = view(where, place.core)
            for step in sorted(range(1, n), key=lambda s: min(s, n - s)):
                coming = dict(where, **{axis: place.along(axis, -step)})
                link, far = direct_link(axis, step, n)
                flow.post(
                    block, block, place.device(axis, step), view(coming, place.core), link, far,
                    lambda went=went, coming=coming: went(coming),
                )
    have(where)


def reduce_flow(flow, place, part, fold, dims, axes, boxes, holds, slims, out, done):
    def stage(k, held, dims):
        axis = axes[k]
        n = place.size[axis]
        spot = dims.index(axis)
        rest = dims[:spot] + dims[spot + 1:]
        box = boxes[k]
        last = k == len(axes) - 1
        target = out if last else holds[k]
        terms, left = [], [n]

        def place_of(step):
            return (slice(None),) * spot + (place.along(axis, step),)

        def finish():
            left[0] -= 1
            if left[0] == 0:
                add_to(target, held.at[place_of(0)], terms)
                if last:
                    done()
                else:
                    stage(k + 1, target, rest)

        def gate(step, then):
            piece = held.at[place_of(step)]
            into = slims[k].at[step - 1] if slims and step else piece
            if k > 0:
                if slims and step:
                    add_to(into, piece, [])
                then(into)
                return
            where = place_of(step) + (slice(None),) * (len(dims) - spot - 1)
            keep, give = part.at[where + (place.core,)], part.at[where + (1 - place.core,)]

            def folded():
                add_to(into, piece, [keep])
                then(into)

            flow.post(give, piece, place.device("core", 1), piece, "core", 0, folded)

        for step in sorted(range(1, n), key=lambda s: -min(s, n - s)):
            slot = box.at[step - 1]
            terms.append(slot)
            link, far = direct_link(axis, step, n)

            def send(src, slot=slot, step=step, link=link, far=far):
                flow.post(src, slot, place.device(axis, step), slot, link, far, finish)

            gate(step, send)
        gate(0, lambda src: finish())

    stage(0, fold, tuple(dims))


def reduce_scratch(sizes, dims, axes, chunk, narrow):
    def buffer(lead, kind=jnp.float32):
        return pltpu.VMEM(tuple(lead) + tuple(chunk), kind)

    kind = jnp.bfloat16 if narrow else jnp.float32
    left = list(dims)
    fold = buffer([sizes[d] for d in left])
    boxes, holds, slims = [], [], []
    for stage, axis in enumerate(axes):
        left.remove(axis)
        part = [sizes[d] for d in left]
        boxes.append(buffer([sizes[axis] - 1] + part, kind))
        if narrow:
            slims.append(buffer([sizes[axis] - 1] + part, kind))
        if stage < len(axes) - 1:
            holds.append(buffer(part))
    return [fold] + boxes + holds + slims


def split_scratch(refs, stages, narrow):
    refs = list(refs)
    fold, boxes, holds = refs[0], refs[1:1 + stages], refs[1 + stages:2 * stages]
    used = 3 * stages if narrow else 2 * stages
    return (fold, boxes, holds, refs[2 * stages:used]), refs[used:]


def reduce_copies(sizes, axes):
    return sizes[axes[0]] + sum(sizes[a] - 1 for a in axes)


def mesh_sizes():
    return {
        "z": lax.axis_size("dp") // CORES,
        "tensor": lax.axis_size("tensor"),
        "corpus": lax.axis_size("corpus"),
    }


def peers(place, axes):
    found = [("core", 1)]
    for axis in axes:
        found += [(axis, step) for step in range(1, place.size[axis])]
    return found


VMEM_SPEC = pl.BlockSpec(memory_space=pltpu.VMEM)


def kernel_call(kernel, outs, scratch, copies, number, inputs):
    return pl.pallas_call(
        kernel,
        out_shape=outs,
        in_specs=[VMEM_SPEC] * len(inputs),
        out_specs=[VMEM_SPEC] * len(outs),
        scratch_shapes=[
            pltpu.SemaphoreType.DMA((copies,)),
            pltpu.SemaphoreType.DMA((copies,)),
        ] + scratch,
        compiler_params=pltpu.CompilerParams(
            collective_id=number, has_side_effects=True, vmem_limit_bytes=VMEM_LIMIT
        ),
    )(*inputs)


def swapper(flow, place, view):
    def swap(where):
        block = view(where, place.core)
        landing = view(where, 1 - place.core)
        flow.post(block, block, place.device("core", 1), landing, "core", 0)
    return swap


def query_kernel(q_in, ids_in, q_out, ids_out, send_sem, recv_sem, own_sem):
    place = Place()
    flow = Flow(send_sem, recv_sem)
    n_t = place.size["tensor"]
    t, c, z, core = place.at["tensor"], place.at["corpus"], place.at["z"], place.core
    place.greet(peers(place, ("z", "corpus", "tensor")))
    keep = [
        pltpu.make_async_copy(q_in.at[t], q_out.at[t, c, z, core], own_sem.at[0]),
        pltpu.make_async_copy(ids_in, ids_out.at[t, c, z, core], own_sem.at[1]),
    ]
    for copy in keep:
        copy.start()
    half = n_t // 2

    def of(ref, part):
        return lambda where, k: ref.at[part, where["corpus"], where["z"], k]

    left = [2 * (n_t - 1)]

    def begin():
        left[0] -= 1
        if left[0]:
            return
        for copy in keep:
            copy.wait()
        for ref, part, axes, ring in (
            (q_out, slice(half, n_t), ("z", "corpus"), True),
            (q_out, slice(0, half), ("corpus", "z"), False),
            (ids_out, slice(0, n_t), ("corpus", "z"), True),
        ):
            view = of(ref, part)
            spread(
                flow, place, view, {"corpus": c, "z": z}, axes, ring, swapper(flow, place, view)
            )

    for step in range(1, n_t):
        peer, source = place.along("tensor", step), place.along("tensor", -step)
        link, far = direct_link("tensor", step, n_t)
        device = place.device("tensor", step)
        flow.post(
            q_in.at[peer], q_out.at[t, c, z, core], device, q_out.at[source, c, z, core],
            link, far, begin,
        )
        flow.post(
            ids_in, ids_out.at[t, c, z, core], device, ids_out.at[source, c, z, core],
            link, far, begin,
        )
    flow.run()


def gather_queries(queries, ids):
    sizes = mesh_sizes()
    n_t, n_c, n_z = sizes["tensor"], sizes["corpus"], sizes["z"]
    qd, feat = queries.shape
    width = feat // n_t
    mine = queries.reshape(qd, n_t, width).swapaxes(0, 1)
    lead = (n_t, n_c, n_z, CORES)
    count = ids.shape[1]
    copies = 2 * (n_t - 1) + 3 * (2 * n_c * n_z - 1)
    every_query, every_id = kernel_call(
        query_kernel,
        [
            jax.ShapeDtypeStruct(lead + (qd, width), queries.dtype),
            jax.ShapeDtypeStruct(lead + (1, count), ids.dtype),
        ],
        [pltpu.SemaphoreType.DMA((2,))], copies, 0, (mine, ids),
    )
    groups, members = n_t * n_c, n_z * CORES
    return (
        every_query.reshape(groups, members * qd, width),
        every_id.reshape(groups, members, count),
    )


def weight_kernel(*refs):
    parts = 3
    ins, outs = refs[:parts], refs[parts:2 * parts]
    send_sem, recv_sem, own_sem = refs[2 * parts:]
    place = Place()
    flow = Flow(send_sem, recv_sem)
    n_t, n_c, n_z = (place.size[a] for a in ("tensor", "corpus", "z"))
    t, c, z, core = place.at["tensor"], place.at["corpus"], place.at["z"], place.core
    plane = [(a, b) for a in range(n_t) for b in range(n_c) if a or b]
    plane.sort(key=lambda o: -(min(o[0], n_t - o[0]) + min(o[1], n_c - o[1])))

    def over(a, b):
        return {"tensor": place.along("tensor", a), "corpus": place.along("corpus", b)}

    barrier = pltpu.get_barrier_semaphore()
    others = [place.device("core", 1)] + [place.device("z", w) for w in range(1, n_z)]
    others += [over(a, b) for a, b in plane]
    for device in others:
        pl.semaphore_signal(
            barrier, inc=1, device_id=device, device_id_type=pl.DeviceIdType.MESH
        )
    pl.semaphore_wait(barrier, len(others))
    keep = [
        pltpu.make_async_copy(i, o.at[t, c, z, core], own_sem.at[n])
        for n, (i, o) in enumerate(zip(ins, outs))
    ]
    for copy in keep:
        copy.start()
    for copy in keep:
        copy.wait()
    here = {"tensor": t, "corpus": c, "z": z}
    every = {"tensor": slice(None), "corpus": slice(None), "z": slice(None)}

    def of(ref):
        return lambda where, k: ref.at[where["tensor"], where["corpus"], where["z"], k]

    def to_plane(view, where, then):
        block = view(where, core)
        for a, b in plane:
            coming = dict(where, **over(-a, -b))
            far = min(a, n_t - a) + min(b, n_c - b)
            link = direct_link("tensor", a, n_t)[0] if a else direct_link("corpus", b, n_c)[0]
            flow.post(
                block, block, over(a, b), view(coming, core), link, far,
                lambda coming=coming: then(coming),
            )

    def around(view, where, have, flip):
        hops = ring_hops(n_z, flip)
        for way in (1, -1):
            if hops[way]:
                relay(flow, place, view, where, "z", way, 0, hops[way], have)

    for ref in outs[1:]:
        view = of(ref)
        swap = swapper(flow, place, view)
        left = [len(plane)]

        def landed(coming, view=view, swap=swap, left=left):
            left[0] -= 1
            if left[0] == 0:
                whole = dict(every, z=z)
                around(view, whole, swap, False)
                swap(whole)

        to_plane(view, here, landed)

    view = of(outs[0])
    swap = swapper(flow, place, view)
    count = [n_z - 1]

    def stacked():
        count[0] -= 1
        if count[0] == 0:
            column = dict(here, z=slice(None))
            to_plane(view, column, swap)
            swap(column)

    for step in range(1, n_z):
        coming = dict(here, z=place.along("z", -step))
        link, far = direct_link("z", step, n_z)
        block = view(here, core)
        flow.post(block, block, place.device("z", step), view(coming, core), link, far, stacked)
    flow.run()


def gather_weights(parts):
    sizes = mesh_sizes()
    n_t, n_c, n_z = sizes["tensor"], sizes["corpus"], sizes["z"]
    lead = (n_t, n_c, n_z, CORES)
    flat = n_t * n_c
    copies = 3 * (flat - 1 + n_z - 1) + 2 * n_z + flat
    return kernel_call(
        weight_kernel,
        [jax.ShapeDtypeStruct(lead + p.shape, p.dtype) for p in parts],
        [pltpu.SemaphoreType.DMA((len(parts),))], copies, 1, tuple(parts),
    )


SCORE_DIMS = ("tensor", "corpus", "z")
SCORE_WALKS = (
    ("tensor", "corpus", "z"),
    ("corpus", "tensor", "z"),
    ("z", "corpus", "tensor"),
)


def score_kernel(*refs):
    parts = len(SCORE_WALKS)
    ins, outs = refs[:parts], refs[parts:2 * parts]
    send_sem, recv_sem = refs[2 * parts:2 * parts + 2]
    scratch = refs[2 * parts + 2:]
    place = Place()
    flow = Flow(send_sem, recv_sem)
    place.greet(peers(place, SCORE_DIMS))
    for n, axes in enumerate(SCORE_WALKS):
        (fold, boxes, holds, slims), scratch = split_scratch(scratch, len(axes), False)
        reduce_flow(
            flow, place, ins[n], fold, SCORE_DIMS, axes, boxes, holds, slims, outs[n],
            lambda: None,
        )
    flow.run()


def scatter_scores(parts):
    sizes = mesh_sizes()
    scratch = []
    chunks = [p.shape[4:] for p in parts]
    for chunk, axes in zip(chunks, SCORE_WALKS):
        scratch += reduce_scratch(sizes, SCORE_DIMS, axes, chunk, False)
    copies = sum(reduce_copies(sizes, axes) for axes in SCORE_WALKS)
    return kernel_call(
        score_kernel, [jax.ShapeDtypeStruct(c, jnp.float32) for c in chunks],
        scratch, copies, 2, tuple(parts),
    )


GRAD_DIMS = ("corpus", "z")


def grad_walks(n_t):
    first = max(1, 3 * n_t // 4)
    return [("corpus", "z")] * first + [("z", "corpus")] * (n_t - first)


def grad_kernel(part, out, send_sem, recv_sem, own_sem, total, *scratch):
    place = Place()
    flow = Flow(send_sem, recv_sem)
    n_t, t = place.size["tensor"], place.at["tensor"]
    place.greet(peers(place, ("corpus", "z", "tensor")))
    left = [n_t]
    keep = pltpu.make_async_copy(total.at[t], out.at[t], own_sem.at[0])

    def done():
        left[0] -= 1
        if left[0]:
            return
        keep.start()
        for step in range(1, n_t):
            peer, source = place.along("tensor", step), place.along("tensor", -step)
            link, far = direct_link("tensor", step, n_t)
            flow.post(
                total.at[peer], out.at[t], place.device("tensor", step), out.at[source], link, far
            )

    walks = grad_walks(n_t)
    order = sorted(range(n_t), key=lambda n: walks[n] != walks[-1])
    slots = []
    for axes in walks:
        held, scratch = split_scratch(scratch, len(axes), True)
        slots.append(held)
    for n in order:
        fold, boxes, holds, slims = slots[n]
        reduce_flow(
            flow, place, part.at[n], fold, GRAD_DIMS, walks[n], boxes, holds, slims,
            total.at[n], done,
        )
    flow.run()
    keep.wait()


def scatter_grads(part):
    sizes = mesh_sizes()
    qd, width = part.shape[4:]
    n_t = sizes["tensor"]
    scratch = [pltpu.SemaphoreType.DMA((1,)), pltpu.VMEM((n_t, qd, width), jnp.float32)]
    copies = n_t - 1
    for axes in grad_walks(n_t):
        scratch += reduce_scratch(sizes, GRAD_DIMS, axes, (qd, width), True)
        copies += reduce_copies(sizes, axes)
    (mine,) = kernel_call(
        grad_kernel, [jax.ShapeDtypeStruct((n_t, qd, width), jnp.float32)],
        scratch, copies, 3, (part,),
    )
    return mine.swapaxes(0, 1).reshape(qd, n_t * width)


def body(queries, passages, pos_ids, neg_ids):
    sizes = mesh_sizes()
    n_t, n_c, n_z = sizes["tensor"], sizes["corpus"], sizes["z"]
    n_dp = n_z * CORES
    qd, feat = queries.shape
    block_rows, width = passages.shape
    neg_count = neg_ids.shape[1]
    n_groups = n_t * n_c
    members = n_dp * qd
    items = (neg_count + 1) * qd
    padded = -(-(items + 1) // 128) * 128
    scale = feat ** (-0.5)
    f32, bf16 = jnp.float32, jnp.bfloat16
    block = lax.axis_index("dp") * n_c + lax.axis_index("corpus")
    lead = (n_t, n_c, n_z, CORES)

    ids = jnp.concatenate([pos_ids[None, :], neg_ids.T], axis=0).reshape(1, items)
    ids = jnp.pad(ids, ((0, 0), (0, padded - items)), constant_values=-1)
    every_query, every_id = gather_queries(queries, ids)

    item_no = jnp.arange(padded, dtype=jnp.int32)
    match = every_id // block_rows == block
    before = (item_no[:, None] < item_no[None, :]).astype(bf16)
    rank = jnp.einsum("gdj,jk->gdk", match.astype(bf16), before, preferred_element_type=f32)
    rank = jnp.where(match, rank.astype(jnp.int32), -1)
    packed = (every_id % block_rows) * padded + item_no + 1
    slot_no = jnp.arange(CAP, dtype=jnp.int32)
    held = jnp.sum(
        jnp.where(rank[:, :, None, :] == slot_no[:, None], packed[:, :, None, :], 0), axis=3
    )
    full = held > 0
    row = jnp.where(full, (held - 1) // padded, -1)
    item = jnp.where(full, (held - 1) % padded, -1)
    slots = n_dp * CAP
    own = jnp.arange(n_dp, dtype=jnp.int32)[:, None] * qd + item % qd
    own = jnp.where(full, own, -1).reshape(n_groups, slots)
    is_pos = (full & (item < qd)).reshape(n_groups, slots)
    member_no = jnp.arange(members, dtype=jnp.int32)
    onehot = (row.reshape(n_groups, slots)[:, :, None] == jnp.arange(block_rows)).astype(bf16)
    at_own = own[:, :, None] == member_no
    pick_pos = (at_own & is_pos[:, :, None]).astype(bf16)
    at_neg = at_own & ~is_pos[:, :, None]

    rows = jnp.einsum("gsp,pw->gsw", onehot, passages, preferred_element_type=f32).astype(bf16)
    pos_rows = jnp.einsum("gsc,gsw->gcw", pick_pos, rows, preferred_element_type=f32).astype(bf16)
    half = members // 2
    in_parts = [
        jnp.einsum("gqw,gcw->gqc", every_query, cols, preferred_element_type=f32)
        for cols in (pos_rows[:, :half], pos_rows[:, half:])
    ]
    slot_part = jnp.einsum("gsw,gqw->gsq", rows, every_query, preferred_element_type=f32)
    score = jnp.sum(jnp.where(at_neg, slot_part, 0.0), axis=2).reshape(n_groups, n_dp, CAP)
    neg_no = item_no[qd:items]
    neg_part = jnp.sum(
        jnp.where(item[:, :, :, None] == neg_no, score[:, :, :, None], 0.0), axis=2
    )
    neg_shape = (neg_count * qd // 128, 128)
    left, right, neg = scatter_scores([
        in_parts[0].reshape(lead + (qd, half)),
        in_parts[1].reshape(lead + (qd, half)),
        neg_part.reshape(lead + neg_shape),
    ])
    neg = neg.reshape(neg_count, qd).T
    logits = jnp.concatenate([left, right, neg], axis=1) * scale

    row_max = jnp.max(logits, axis=1, keepdims=True)
    exponent = jnp.exp(logits - row_max)
    denominator = jnp.sum(exponent, axis=1, keepdims=True)
    own_col = lax.axis_index("dp") * qd + jnp.arange(qd)
    target = (jnp.arange(members + neg_count)[None, :] == own_col[:, None]).astype(f32)
    losses = jnp.log(denominator[:, 0]) + row_max[:, 0] - jnp.sum(target * logits, axis=1)
    weights = (exponent / denominator - target).astype(bf16)

    left, right, neg = gather_weights([
        weights[:, :half],
        weights[:, half:members],
        weights[:, members:].T.astype(f32).reshape(neg_shape),
    ])
    neg_weights = neg.reshape(n_groups, n_dp, 1, neg_count * qd)
    slot_weight = jnp.sum(
        jnp.where(item[:, :, :, None] == neg_no, neg_weights, 0.0), axis=3
    ).reshape(n_groups, slots)
    mixed = sum(
        jnp.einsum(
            "gsc,gqc->gsq", pick, w.reshape(n_groups, members, half), preferred_element_type=f32
        )
        for pick, w in ((pick_pos[..., :half], left), (pick_pos[..., half:], right))
    )
    mixed = jnp.where(at_neg, slot_weight[:, :, None], mixed).astype(bf16)
    query_part = jnp.einsum("gsq,gsw->gqw", mixed, rows, preferred_element_type=f32) * scale
    grad_query = scatter_grads(query_part.reshape(lead + (qd, width)))
    slot_grads = jnp.einsum("gsq,gqw->gsw", mixed, every_query, preferred_element_type=f32)
    slot_grads = (slot_grads * scale).astype(bf16)
    grad_pass = jnp.einsum("gsp,gsw->pw", onehot, slot_grads, preferred_element_type=f32)
    return (grad_query, losses, grad_pass)


def solution(mesh):
    in_specs = (
        P(("dp", "tensor", "corpus"), None),
        P(("dp", "corpus"), "tensor"),
        P(("dp", "tensor", "corpus")),
        P(("dp", "tensor", "corpus"), None),
    )
    out_specs = (
        P(("dp", "tensor", "corpus"), None),
        P(("dp", "tensor", "corpus")),
        P(("dp", "corpus"), "tensor"),
    )
    return jax.shard_map(body, mesh=mesh, in_specs=in_specs, out_specs=out_specs, check_vma=False)
```
